32 devices in a mesh: dp: 2 (over x), ind: 4 (over z), probe: 4 (over y, core).
Axes of the slice: x: 2, y: 2, z: 4, core: 2. Of those that a mesh axis runs over, the one named last changes fastest.
Arguments:
- data_x: bfloat16 [16, 1024], P(None, 'dp'), may hold values from -6 to 6
- inducing_z: bfloat16 [16, 65536], P(None, 'ind'), may hold values from -6 to 6
- lengthscale: float32 [16], replicated, may hold values from 1.5 to 3
- noise_var: float32 [1], replicated, may hold values from 0.5 to 2
- solves: bfloat16 [32, 65536], P('probe', 'ind'), may hold values from -0.09375 to 0.09375
- probe_signs: int32 [32, 65536], P('probe', 'ind'), may hold values 0 or 1
Outputs:
- grad_z: float32 [16, 65536], P(None, 'ind')
The draws below stay inside these ranges and needn't reach their ends.
All inputs are finite; a program needn't handle non-finite values. No bound on the sum of `probe_signs` on one device may be relied on, other than what follows from the above.
Results may differ from the reference program's by a relative error of at most 0.0095.
Values may be sent and summed in bfloat16 or wider, within the bound.
No kernel may reach another device: no remote copies, remote signals or barrier semaphores. Data moves between devices by JAX's collectives and lax.ppermute only.
A program may use at most 64 MiB of HBM per device.

```python
import math
import jax
import jax.numpy as jnp
from jax import lax

DIM = 16
M = 65536
P_SIZE = 32
N = 1024


def with_ends(values, rng, least, high):
    shape = values.shape
    place = [jax.random.randint(jax.random.fold_in(rng, axis), (), 0, shape[axis]) for axis in range(len(shape))]
    values = values.at[tuple(place)].set(least)
    longest = shape.index(max(shape))
    place[longest] = (place[longest] + 1) % shape[longest]
    return values.at[tuple(place)].set(high)


def block_levels(own_key, extent, cuts, smallest, high):
    loudness = 1.0
    for position, blocks in cuts:
        steps = jax.random.uniform(jax.random.fold_in(jax.random.fold_in(own_key, 6), position), (blocks,), jnp.float32, smallest / len(cuts), high / len(cuts))
        loudness = loudness * jnp.repeat(jnp.exp(steps), extent[position] // blocks).reshape((-1,) + (1,) * (len(extent) - 1 - position))
    return loudness


def normal_values(own_key, extent, deviation, bound, shards=(), held_as=jnp.bfloat16):
    result = deviation * jax.random.normal(own_key, extent, jnp.float32)
    if shards:
        result = result * block_levels(own_key, extent, shards, -0.22, 0.18)
    return jnp.clip(result, -bound, bound).astype(held_as)


def setup_inputs(seed: int = 0) -> dict:
    seeds = jax.random.split(jax.random.key(seed), 7)
    return {
        "data_x": normal_values(seeds[0], (DIM, N), 1.0, 6.0, ((1, 2),)),
        "inducing_z": normal_values(seeds[1], (DIM, M), 1.0, 6.0, ((1, 4),)),
        "lengthscale": jnp.clip(jnp.exp(jax.random.uniform(seeds[2], (DIM,), jnp.float32, math.log(1.5), math.log(3.0))), 1.5, 3.0),
        "noise_var": jnp.clip(jnp.exp(jax.random.uniform(seeds[3], (1,), jnp.float32, math.log(0.5), math.log(2.0))), 0.5, 2.0),
        "solves": normal_values(seeds[4], (P_SIZE, M), 4096 ** -0.5, 0.09375, ((0, 4), (1, 4))),
        "probe_signs": with_ends((jax.random.randint(seeds[5], (P_SIZE, M), 0, 2) < 1).astype(jnp.int32), jax.random.fold_in(seeds[5], 1), 0, 1),
    }


def kernel_block(x_scaled, x_square, z_scaled, z_square):
    cross = lax.dot_general(x_scaled, z_scaled, (((0,), (0,)), ((), ())), preferred_element_type=jnp.float32)
    dist = x_square[:, None] + z_square[None, :] - 2.0 * cross
    return jnp.exp(-0.5 * dist).astype(jnp.bfloat16)


def reference(data_x, inducing_z, lengthscale, noise_var, solves, probe_signs):
    inverse = (1.0 / lengthscale).astype(jnp.float32)
    x_scaled = (data_x.astype(jnp.float32) * inverse[:, None]).astype(jnp.bfloat16)
    z_scaled = (inducing_z.astype(jnp.float32) * inverse[:, None]).astype(jnp.bfloat16)
    x_wide = x_scaled.astype(jnp.float32)
    z_wide = z_scaled.astype(jnp.float32)
    x_square = jnp.sum(x_wide * x_wide, axis=0)
    z_square = jnp.sum(z_wide * z_wide, axis=0)
    probe_vals = (2 * probe_signs - 1).astype(jnp.bfloat16)
    stacked = jnp.concatenate([solves, probe_vals], axis=0)
    total_cols = z_scaled.shape[1]
    block_cols = min(2048, total_cols)
    blocks_count = total_cols // block_cols
    rows_count = x_scaled.shape[1]

    def first_pass(col_index, totals):
        start = (col_index * block_cols).astype(jnp.int32)
        z_part = lax.dynamic_slice_in_dim(z_scaled, start, block_cols, 1)
        zsq_part = lax.dynamic_slice_in_dim(z_square, start, block_cols, 0)
        kern = kernel_block(x_scaled, x_square, z_part, zsq_part)
        stack_part = lax.dynamic_slice_in_dim(stacked, start, block_cols, 1)
        return totals + lax.dot_general(stack_part, kern, (((1,), (1,)), ((), ())), preferred_element_type=jnp.float32)

    projections = lax.fori_loop(0, blocks_count, first_pass, jnp.zeros((2 * P_SIZE, rows_count), jnp.float32))
    proj_round = projections.astype(jnp.bfloat16)
    swapped = jnp.concatenate([proj_round[P_SIZE:], proj_round[:P_SIZE]], axis=0)

    def second_pass(col_index):
        start = (col_index * block_cols).astype(jnp.int32)
        z_part = lax.dynamic_slice_in_dim(z_scaled, start, block_cols, 1)
        zsq_part = lax.dynamic_slice_in_dim(z_square, start, block_cols, 0)
        kern = kernel_block(x_scaled, x_square, z_part, zsq_part)
        stack_part = lax.dynamic_slice_in_dim(stacked, start, block_cols, 1)
        coef = lax.dot_general(swapped, stack_part, (((0,), (0,)), ((), ())), preferred_element_type=jnp.float32)
        weighted = (kern.astype(jnp.float32) * coef).astype(jnp.bfloat16)
        moment = jnp.dot(data_x, weighted, preferred_element_type=jnp.float32)
        row_total = jnp.sum(weighted, axis=0, dtype=jnp.float32)
        z_raw = lax.dynamic_slice_in_dim(inducing_z, start, block_cols, 1).astype(jnp.float32)
        return moment - z_raw * row_total[None, :]

    pieces = lax.map(second_pass, jnp.arange(blocks_count, dtype=jnp.int32))
    gathered = jnp.transpose(pieces, (1, 0, 2)).reshape(DIM, total_cols)
    factor = inverse * inverse / (noise_var[0] * P_SIZE)
    return gathered * factor[:, None]
```

```python
import functools
import math

import jax
import jax.numpy as jnp
from jax import lax
from jax.experimental import pallas as pl
from jax.experimental.pallas import tpu as pltpu
from jax.sharding import PartitionSpec as P

LOG2E = math.log2(math.e)
F32 = jnp.float32
BF16 = jnp.bfloat16
VMEM = pl.BlockSpec(memory_space=pltpu.VMEM)
SMEM = pl.BlockSpec(memory_space=pltpu.SMEM)
K_ROWS = 64


def tile_of(extent, limit):
    tile = min(extent, limit)
    while extent % tile:
        tile //= 2
    return tile


def column(row):
    d = row.shape[1]
    spread = jnp.broadcast_to(row, (d, d))
    eye = lax.broadcasted_iota(jnp.int32, (d, d), 0) == lax.broadcasted_iota(jnp.int32, (d, d), 1)
    return jnp.sum(jnp.where(eye, spread, 0.0), axis=1, keepdims=True)


def split3(value):
    high = value.astype(BF16).astype(F32)
    rest = value - high
    middle = rest.astype(BF16).astype(F32)
    return high, middle, rest - middle


def padded(parts):
    rows = jnp.concatenate(parts, axis=0)
    return jnp.concatenate([rows, jnp.zeros((K_ROWS - rows.shape[0], rows.shape[1]), F32)], axis=0)


def x_side(x, inverse):
    wide = (x.astype(F32) * inverse).astype(BF16).astype(F32)
    square = jnp.sum(wide * wide, axis=0, keepdims=True) * (-0.5 * LOG2E)
    ones = jnp.ones((3, x.shape[1]), F32)
    return jnp.transpose(padded([*split3(wide * LOG2E), *split3(square), ones])).astype(BF16)


def z_side(z, inverse):
    wide = (z.astype(F32) * inverse).astype(BF16).astype(F32)
    square = jnp.sum(wide * wide, axis=0, keepdims=True) * (-0.5 * LOG2E)
    ones = jnp.ones((3, z.shape[1]), F32)
    return padded([wide, wide, wide, ones, *split3(square)]).astype(BF16)


def kern_body(tile, place_ref, length_ref, x_ref, z_ref, kern_ref):
    inverse = column(1.0 / length_ref[...])
    left = x_side(x_ref[...], inverse)
    columns = kern_ref.shape[1]
    first = place_ref[0] * columns

    def step(index, carry):
        source = pl.ds(pl.multiple_of(first + index * tile, tile), tile)
        target = pl.ds(pl.multiple_of(index * tile, tile), tile)
        right = z_side(z_ref[:, source], inverse)
        kern_ref[:, target] = jnp.exp2(jnp.dot(left, right, preferred_element_type=F32)).astype(BF16)
        return carry

    lax.fori_loop(0, columns // tile, step, 0)


def kern_call(place, length, x, z, columns):
    rows = x.shape[1]
    return pl.pallas_call(
        functools.partial(kern_body, tile_of(columns, 2048)),
        out_shape=pltpu.VMEM((rows, columns), BF16),
        in_specs=[SMEM, VMEM, VMEM, VMEM],
        out_specs=VMEM,
        compiler_params=pltpu.CompilerParams(vmem_limit_bytes=24 << 20),
        cost_estimate=pl.CostEstimate(
            flops=2 * rows * columns * K_ROWS, bytes_accessed=2 * rows * columns, transcendentals=rows * columns
        ),
        name="kern",
    )(place, length, x, z)


def project_body(tile, place_ref, kern_ref, solves_ref, signs_ref, solves2_ref, signs2_ref, stack_ref, own_ref, other_ref):
    columns = kern_ref.shape[1]
    first = place_ref[0] * columns
    total = None
    for index in range(columns // tile):
        source = pl.ds(pl.multiple_of(first + index * tile, tile), tile)
        target = slice(index * tile, (index + 1) * tile)
        part = jnp.concatenate(
            [
                solves_ref[:, source].astype(F32),
                (2 * signs_ref[:, source] - 1).astype(F32),
                solves2_ref[:, source].astype(F32),
                (2 * signs2_ref[:, source] - 1).astype(F32),
            ],
            axis=0,
        ).astype(BF16)
        stack_ref[:, target] = part
        term = lax.dot_general(kern_ref[:, target], part, (((1,), (1,)), ((), ())), preferred_element_type=F32)
        total = term if total is None else total + term
    total = jnp.transpose(total)
    half = total.shape[0] // 2
    own_ref[...] = total[:half]
    other_ref[...] = total[half:].astype(BF16)


def project_call(place, kern, solves, signs, solves2, signs2):
    rows, columns = kern.shape
    probes = solves.shape[0]
    return pl.pallas_call(
        functools.partial(project_body, tile_of(columns, 2048)),
        out_shape=(
            jax.ShapeDtypeStruct((4 * probes, columns), BF16),
            jax.ShapeDtypeStruct((2 * probes, rows), F32),
            jax.ShapeDtypeStruct((2 * probes, rows), BF16),
        ),
        in_specs=[SMEM] + [VMEM] * 5,
        out_specs=(VMEM,) * 3,
        compiler_params=pltpu.CompilerParams(vmem_limit_bytes=24 << 20),
        cost_estimate=pl.CostEstimate(
            flops=8 * rows * columns * probes, bytes_accessed=2 * rows * columns, transcendentals=0
        ),
        name="project",
    )(place, kern, solves, signs, solves2, signs2)


def gradient_body(
    tile, groups, halves, p_size, place_ref, noise_ref, length_ref, z_ref, stacks, projections, data, kerns, grad_ref
):
    core, group = place_ref[0], place_ref[1]
    columns = grad_ref.shape[1]
    first = core * columns
    inverse = column(1.0 / length_ref[...])
    factor = inverse * inverse / (noise_ref[0] * p_size)

    def in_order(values):
        if groups != 2:
            return values
        own, other = values
        return [jnp.where(group == 0, own, other), jnp.where(group == 0, other, own)]

    lefts, rows = [], []
    for half in range(halves):
        blocks = []
        for index in range(groups):
            parts = []
            for block in (projections[0], projections[1]):
                value = block[half * groups + index].astype(F32)
                middle = value.shape[0] // 2
                parts += [value[middle:], value[:middle]]
            blocks.append(jnp.concatenate(parts, axis=0))
        lefts.append(jnp.transpose(jnp.concatenate(in_order(blocks), axis=0)).astype(BF16))
        x = data[half][...].astype(F32)
        rows.append(jnp.concatenate([x, jnp.ones((16, x.shape[1]), F32)], axis=0).astype(BF16))
    dims = data[0].shape[0]

    def step(index, carry):
        source = pl.ds(pl.multiple_of(first + index * tile, tile), tile)
        target = pl.ds(pl.multiple_of(index * tile, tile), tile)
        stack = jnp.concatenate(in_order([ref[:, target].astype(F32) for ref in stacks]), axis=0).astype(BF16)
        total = None
        for half in range(halves):
            coef = jnp.dot(lefts[half], stack, preferred_element_type=F32)
            weighted = (kerns[half][:, target].astype(F32) * coef).astype(BF16)
            term = jnp.dot(rows[half], weighted, preferred_element_type=F32)
            total = term if total is None else total + term
        z = z_ref[:, source].astype(F32)
        grad_ref[:, target] = ((total[:dims] - z * total[dims : dims + 1]) * factor).astype(grad_ref.dtype)
        return carry

    lax.fori_loop(0, columns // tile, step, 0)


def gradient_call(place, noise, length, z, stacks, projections, data, kerns, p_size, dtype):
    rows, columns = kerns[0].shape
    groups, halves = len(stacks), len(kerns)

    def body(place_ref, noise_ref, length_ref, z_ref, *refs):
        refs = list(refs)
        take = lambda count: [refs.pop(0) for _ in range(count)]
        stack_refs, projection_refs, data_refs, kern_refs = take(groups), take(2), take(halves), take(halves)
        gradient_body(
            tile_of(columns, 1024), groups, halves, p_size, place_ref, noise_ref, length_ref, z_ref,
            stack_refs, projection_refs, data_refs, kern_refs, refs[0],
        )

    return pl.pallas_call(
        body,
        out_shape=jax.ShapeDtypeStruct((z.shape[0], columns), dtype),
        in_specs=[SMEM, SMEM] + [VMEM] * (2 + groups + 2 + 2 * halves),
        out_specs=VMEM,
        compiler_params=pltpu.CompilerParams(vmem_limit_bytes=32 << 20),
        cost_estimate=pl.CostEstimate(
            flops=2 * halves * rows * columns * 128, bytes_accessed=2 * halves * rows * columns, transcendentals=0
        ),
        name="gradient",
    )(place, noise, length, z, *stacks, *projections, *data, *kerns)


def solution(mesh):
    dp, ind, probe = mesh.shape["dp"], mesh.shape["ind"], mesh.shape["probe"]
    groups = probe // 2
    halves = dp if dp <= 2 else 1
    core_swap = [(i, i ^ 1) for i in range(probe)]

    def cores(value):
        return lax.ppermute(value, "probe", core_swap)

    def from_group(shift):
        return [((i + 2 * shift) % probe, i) for i in range(probe)]

    def on_device(data_x, inducing_z, lengthscale, noise_var, solves, probe_signs):
        columns = inducing_z.shape[1] // 2
        p_size = solves.shape[0] * probe
        place_index = lax.axis_index("probe")
        place = jnp.stack([place_index % 2, place_index // 2]).astype(jnp.int32)
        length = lengthscale.reshape(1, -1)

        solves2, signs2 = cores(solves), cores(probe_signs)
        data = [data_x] + [lax.ppermute(data_x, "dp", [(i, 1 - i) for i in range(dp)]) for _ in range(halves - 1)]
        kerns = [kern_call(place, length, data_x, inducing_z, columns)]
        stack, own, other = project_call(place, kerns[0], solves, probe_signs, solves2, signs2)
        stacks = [stack] + [lax.ppermute(stack, "probe", from_group(s)) for s in range(1, groups)]
        kerns += [kern_call(place, length, x, inducing_z, columns) for x in data[1:]]

        part = (own + cores(other).astype(F32)).astype(BF16)
        peers = [lax.ppermute(part, "ind", [((i ^ s), i) for i in range(ind)]) for s in range(1, ind)]
        block = sum([p.astype(F32) for p in peers], part.astype(F32)).astype(BF16)

        blocks = []
        for half in range(halves):
            for shift in range(groups):
                pairs = []
                for d in range(dp):
                    for source, target in from_group(shift):
                        pairs.append(((d ^ half) * probe + source, d * probe + target))
                blocks.append(block if half == 0 and shift == 0 else lax.ppermute(block, ("dp", "probe"), pairs))
        own_blocks = jnp.stack(blocks)
        other_blocks = cores(own_blocks)

        whole = halves == dp
        grad = gradient_call(
            place, noise_var, length, inducing_z, stacks, (own_blocks, other_blocks), data, kerns, p_size,
            BF16 if whole else F32,
        )
        if not whole:
            grad = lax.psum(grad, "dp").astype(BF16)
        far = cores(grad)
        lower = place[0] == 0
        return jnp.concatenate(
            [jnp.where(lower, grad, far).astype(F32), jnp.where(lower, far, grad).astype(F32)], axis=1
        )

    return jax.shard_map(
        on_device,
        mesh=mesh,
        in_specs=(P(None, "dp"), P(None, "ind"), P(), P(), P("probe", "ind"), P("probe", "ind")),
        out_specs=P(None, "ind"),
        check_vma=False,
    )
```

```python
import functools
import math

import jax
import jax.numpy as jnp
from jax import lax
from jax.experimental import pallas as pl
from jax.experimental.pallas import tpu as pltpu
from jax.sharding import PartitionSpec as P

LOG2E = math.log2(math.e)
F32 = jnp.float32
BF16 = jnp.bfloat16
VMEM = pl.BlockSpec(memory_space=pltpu.VMEM)
HBM = pl.BlockSpec(memory_space=pltpu.HBM)
SMEM = pl.BlockSpec(memory_space=pltpu.SMEM)
K_ROWS = 128


def tile_of(extent, limit):
    tile = min(extent, limit)
    while extent % tile:
        tile //= 2
    return tile


def column(row):
    d = row.shape[1]
    spread = jnp.broadcast_to(row, (d, d))
    eye = lax.broadcasted_iota(jnp.int32, (d, d), 0) == lax.broadcasted_iota(jnp.int32, (d, d), 1)
    return jnp.sum(jnp.where(eye, spread, 0.0), axis=1, keepdims=True)


def split3(value):
    high = value.astype(BF16).astype(F32)
    rest = value - high
    middle = rest.astype(BF16).astype(F32)
    return high, middle, rest - middle


def padded(parts):
    rows = jnp.concatenate(parts, axis=0)
    return jnp.concatenate([rows, jnp.zeros((K_ROWS - rows.shape[0], rows.shape[1]), F32)], axis=0)


def x_side(x, inverse):
    wide = (x.astype(F32) * inverse).astype(BF16).astype(F32)
    square = jnp.sum(wide * wide, axis=0, keepdims=True) * (-0.5 * LOG2E)
    ones = jnp.ones((3, x.shape[1]), F32)
    return jnp.transpose(padded([*split3(wide * LOG2E), *split3(square), ones])).astype(BF16)


def z_side(z, inverse):
    wide = (z.astype(F32) * inverse).astype(BF16).astype(F32)
    square = jnp.sum(wide * wide, axis=0, keepdims=True) * (-0.5 * LOG2E)
    ones = jnp.ones((3, z.shape[1]), F32)
    return padded([wide, wide, wide, ones, *split3(square)]).astype(BF16)


def stacked(solves, signs):
    return jnp.concatenate([solves.astype(F32), (2 * signs - 1).astype(F32)], axis=0).astype(BF16)


def kern_tiles(tile, inverse, x, z_ref, kern_ref, arrived):
    left = x_side(x, inverse)
    for index in range(kern_ref.shape[1] // tile):
        arrived(index)
        target = slice(index * tile, (index + 1) * tile)
        right = z_side(z_ref[:, target], inverse)
        kern_ref[:, target] = jnp.exp2(jnp.dot(left, right, preferred_element_type=F32)).astype(BF16)


def near_body(
    tile, place_ref, length_hbm, x_hbm, z_hbm, solves_hbm, signs_hbm,
    kern_ref, z_ref, stack_ref, length_ref, x_ref, solves_ref, signs_ref, sems,
):
    columns = kern_ref.shape[1]
    first = place_ref[0] * columns
    whole = pl.ds(pl.multiple_of(first, columns), columns)
    starts = range(0, columns, tile)
    copies = [
        pltpu.make_async_copy(length_hbm, length_ref, sems.at[0]),
        pltpu.make_async_copy(x_hbm, x_ref, sems.at[1]),
    ]
    for index, start in enumerate(starts):
        source = pl.ds(pl.multiple_of(first + start, tile), tile)
        copies.append(pltpu.make_async_copy(z_hbm.at[:, source], z_ref.at[:, pl.ds(start, tile)], sems.at[4 + index]))
    copies.append(pltpu.make_async_copy(solves_hbm.at[:, whole], solves_ref, sems.at[2]))
    copies.append(pltpu.make_async_copy(signs_hbm.at[:, whole], signs_ref, sems.at[3]))
    for copy in copies:
        copy.start()
    copies[0].wait()
    copies[1].wait()
    inverse = column(1.0 / length_ref[...])
    kern_tiles(tile, inverse, x_ref[...], z_ref, kern_ref, lambda index: copies[2 + index].wait())
    copies[-2].wait()
    copies[-1].wait()
    for start in starts:
        target = slice(start, start + tile)
        stack_ref[:, target] = stacked(solves_ref[:, target], signs_ref[:, target])


def far_body(tile, length_ref, x_ref, z_ref, kern_ref):
    kern_tiles(tile, column(1.0 / length_ref[...]), x_ref[...], z_ref, kern_ref, lambda index: None)


def kern_cost(rows, columns):
    return pl.CostEstimate(
        flops=2 * rows * columns * K_ROWS, bytes_accessed=2 * rows * columns, transcendentals=rows * columns
    )


def near_call(place, length, x, z, solves, signs, columns):
    rows, probes = x.shape[1], solves.shape[0]
    tile = tile_of(columns, 2048)
    operands = [pltpu.with_memory_space_constraint(value, pltpu.HBM) for value in (length, x, z, solves, signs)]
    return pl.pallas_call(
        functools.partial(near_body, tile),
        out_shape=(
            pltpu.VMEM((rows, columns), BF16),
            pltpu.VMEM((z.shape[0], columns), z.dtype),
            pltpu.VMEM((2 * probes, columns), BF16),
        ),
        in_specs=[SMEM] + [HBM] * 5,
        out_specs=(VMEM,) * 3,
        scratch_shapes=[
            pltpu.VMEM(length.shape, length.dtype),
            pltpu.VMEM(x.shape, x.dtype),
            pltpu.VMEM((probes, columns), solves.dtype),
            pltpu.VMEM((probes, columns), signs.dtype),
            pltpu.SemaphoreType.DMA((4 + columns // tile,)),
        ],
        compiler_params=pltpu.CompilerParams(vmem_limit_bytes=24 << 20),
        cost_estimate=kern_cost(rows, columns),
        name="kern_near",
    )(place, *operands)


def far_call(length, x, z):
    rows, columns = x.shape[1], z.shape[1]
    return pl.pallas_call(
        functools.partial(far_body, tile_of(columns, 2048)),
        out_shape=pltpu.VMEM((rows, columns), BF16),
        in_specs=[VMEM] * 3,
        out_specs=VMEM,
        compiler_params=pltpu.CompilerParams(vmem_limit_bytes=24 << 20),
        cost_estimate=kern_cost(rows, columns),
        name="kern_far",
    )(length, x, z)


def stack_body(tile, place_ref, near_ref, solves_ref, signs_ref, stack_ref):
    columns = stack_ref.shape[1]
    first = place_ref[0] * columns
    for start in range(0, columns, tile):
        source = pl.ds(pl.multiple_of(first + start, tile), tile)
        target = slice(start, start + tile)
        far = stacked(solves_ref[:, source], signs_ref[:, source])
        stack_ref[:, target] = jnp.concatenate([near_ref[:, target], far], axis=0)


def stack_call(place, near, solves2, signs2):
    rows, columns = near.shape
    return pl.pallas_call(
        functools.partial(stack_body, tile_of(columns, 2048)),
        out_shape=jax.ShapeDtypeStruct((2 * rows, columns), BF16),
        in_specs=[SMEM] + [VMEM] * 3,
        out_specs=VMEM,
        compiler_params=pltpu.CompilerParams(vmem_limit_bytes=16 << 20),
        cost_estimate=pl.CostEstimate(flops=4 * rows * columns, bytes_accessed=8 * rows * columns, transcendentals=0),
        name="stack",
    )(place, near, solves2, signs2)


def project_body(tile, kern_ref, stack_ref, own_ref, other_ref):
    total = None
    for start in range(0, kern_ref.shape[1], tile):
        target = slice(start, start + tile)
        term = lax.dot_general(
            kern_ref[:, target], stack_ref[:, target], (((1,), (1,)), ((), ())), preferred_element_type=F32
        )
        total = term if total is None else total + term
    total = jnp.transpose(total)
    half = total.shape[0] // 2
    own_ref[...] = total[:half]
    other_ref[...] = total[half:].astype(BF16)


def project_call(kern, stack):
    rows, columns = kern.shape
    half = stack.shape[0] // 2
    return pl.pallas_call(
        functools.partial(project_body, tile_of(columns, 2048)),
        out_shape=(jax.ShapeDtypeStruct((half, rows), F32), jax.ShapeDtypeStruct((half, rows), BF16)),
        in_specs=[VMEM] * 2,
        out_specs=(VMEM,) * 2,
        compiler_params=pltpu.CompilerParams(vmem_limit_bytes=24 << 20),
        cost_estimate=pl.CostEstimate(
            flops=4 * rows * columns * half, bytes_accessed=2 * rows * columns, transcendentals=0
        ),
        name="project",
    )(kern, stack)


def gradient_body(
    tile, p_size, group_ref, noise_ref, length_ref, z_ref, stacks, projections, data, kerns, grad_ref, weighted_ref
):
    group = group_ref[1]
    groups, halves = len(stacks), len(kerns)
    columns = grad_ref.shape[1]
    count = kerns[0].shape[0]
    dims = data[0].shape[0]
    inverse = column(1.0 / length_ref[...])
    factor = inverse * inverse / (noise_ref[0] * p_size)

    def in_order(values):
        if groups != 2:
            return values
        own, other = values
        return [jnp.where(group == 0, own, other), jnp.where(group == 0, other, own)]

    lefts, rows = [], []
    for half in range(halves):
        blocks = []
        for index in range(groups):
            parts = []
            for block in projections:
                value = block[half * groups + index].astype(F32)
                middle = value.shape[0] // 2
                parts += [value[middle:], value[:middle]]
            blocks.append(jnp.concatenate(parts, axis=0))
        lefts.append(jnp.transpose(jnp.concatenate(in_order(blocks), axis=0)).astype(BF16))
        x = data[half][...].astype(F32)
        rows.append(jnp.concatenate([x, jnp.ones((16, x.shape[1]), F32)], axis=0).astype(BF16))

    def weigh(index):
        target = slice(index * tile, (index + 1) * tile)
        stack = jnp.concatenate(in_order([ref[:, target].astype(F32) for ref in stacks]), axis=0).astype(BF16)
        for half in range(halves):
            coef = jnp.dot(lefts[half], stack, preferred_element_type=F32)
            weighted = (kerns[half][:, target].astype(F32) * coef).astype(BF16)
            weighted_ref[index % 2, half * count : (half + 1) * count, :] = weighted

    def reduce(index):
        target = slice(index * tile, (index + 1) * tile)
        total = None
        for half in range(halves):
            weighted = weighted_ref[index % 2, half * count : (half + 1) * count, :]
            term = jnp.dot(rows[half], weighted, preferred_element_type=F32)
            total = term if total is None else total + term
        z = z_ref[:, target].astype(F32)
        grad_ref[:, target] = ((total[:dims] - z * total[dims : dims + 1]) * factor).astype(grad_ref.dtype)

    tiles = columns // tile
    for index in range(tiles + 1):
        if index < tiles:
            weigh(index)
        if index > 0:
            reduce(index - 1)


def gradient_call(place, noise, length, z, stacks, projections, data, kerns, p_size, dtype):
    rows, columns = kerns[0].shape
    groups, halves = len(stacks), len(kerns)
    tile = tile_of(columns, 256)

    def body(place_ref, noise_ref, length_ref, z_ref, *refs):
        refs = list(refs)
        take = lambda size: [refs.pop(0) for _ in range(size)]
        stack_refs, projection_refs, data_refs, kern_refs = take(groups), take(2), take(halves), take(halves)
        gradient_body(
            tile, p_size, place_ref, noise_ref, length_ref, z_ref,
            stack_refs, projection_refs, data_refs, kern_refs, *refs,
        )

    return pl.pallas_call(
        body,
        out_shape=jax.ShapeDtypeStruct(z.shape, dtype),
        in_specs=[SMEM, SMEM] + [VMEM] * (2 + groups + 2 + 2 * halves),
        out_specs=VMEM,
        scratch_shapes=[pltpu.VMEM((2, halves * rows, tile), BF16)],
        compiler_params=pltpu.CompilerParams(vmem_limit_bytes=24 << 20),
        cost_estimate=pl.CostEstimate(
            flops=2 * halves * rows * columns * 128, bytes_accessed=2 * halves * rows * columns, transcendentals=0
        ),
        name="gradient",
    )(place, noise, length, z, *stacks, *projections, *data, *kerns)


def solution(mesh):
    dp, ind, probe = mesh.shape["dp"], mesh.shape["ind"], mesh.shape["probe"]
    groups = probe // 2
    halves = dp if dp <= 2 else 1
    core_swap = [(i, i ^ 1) for i in range(probe)]
    pairwise = ind & (ind - 1) == 0

    def cores(value):
        return lax.ppermute(value, "probe", core_swap)

    def from_group(shift):
        return [((i + 2 * shift) % probe, i) for i in range(probe)]

    def from_ind(shift):
        return [(i ^ shift if pairwise else (i + shift) % ind, i) for i in range(ind)]

    def on_device(data_x, inducing_z, lengthscale, noise_var, solves, probe_signs):
        columns = inducing_z.shape[1] // 2
        p_size = solves.shape[0] * probe
        place_index = lax.axis_index("probe")
        place = jnp.stack([place_index % 2, place_index // 2]).astype(jnp.int32)
        length = lengthscale.reshape(1, -1)

        solves2, signs2 = cores(solves), cores(probe_signs)
        data = [data_x]
        for _ in range(halves - 1):
            data.append(lax.ppermute(data_x, "dp", [(i, 1 - i) for i in range(dp)]))
        kern, z, near = near_call(place, length, data_x, inducing_z, solves, probe_signs, columns)
        kerns = [kern]
        stack = stack_call(place, near, solves2, signs2)
        stacks = [stack]
        for shift in range(1, groups):
            stacks.append(lax.ppermute(stack, "probe", from_group(shift)))
        own, other = project_call(kern, stack)
        for x in data[1:]:
            kerns.append(far_call(length, x, z))

        part = (own + cores(other).astype(F32)).astype(BF16)
        peers = []
        for shift in range(1, ind):
            peers.append(lax.ppermute(part, "ind", from_ind(shift)))
        block = sum([p.astype(F32) for p in peers], part.astype(F32)).astype(BF16)

        blocks = []
        for half in range(halves):
            for shift in range(groups):
                pairs = []
                for d in range(dp):
                    for source, target in from_group(shift):
                        pairs.append(((d ^ half) * probe + source, d * probe + target))
                blocks.append(block if half == 0 and shift == 0 else lax.ppermute(block, ("dp", "probe"), pairs))
        own_blocks = jnp.stack(blocks)
        other_blocks = cores(own_blocks)

        whole = halves == dp
        grad = gradient_call(
            place, noise_var, length, z, stacks, (own_blocks, other_blocks), data, kerns, p_size,
            BF16 if whole else F32,
        )
        if not whole:
            grad = lax.psum(grad, "dp").astype(BF16)
        far = cores(grad)
        lower = place[0] == 0
        return jnp.concatenate(
            [jnp.where(lower, grad, far).astype(F32), jnp.where(lower, far, grad).astype(F32)], axis=1
        )

    return jax.shard_map(
        on_device,
        mesh=mesh,
        in_specs=(P(None, "dp"), P(None, "ind"), P(), P(), P("probe", "ind"), P("probe", "ind")),
        out_specs=P(None, "ind"),
        check_vma=False,
    )
```

```python
import functools
import math

import jax
import jax.numpy as jnp
from jax import lax
from jax.experimental import pallas as pl
from jax.experimental.pallas import tpu as pltpu
from jax.sharding import PartitionSpec as P

LOG2E = math.log2(math.e)
F32 = jnp.float32
BF16 = jnp.bfloat16
VMEM = pl.BlockSpec(memory_space=pltpu.VMEM)
HBM = pl.BlockSpec(memory_space=pltpu.HBM)
K_ROWS = 128


def tile_of(extent, limit):
    tile = min(extent, limit)
    while extent % tile:
        tile //= 2
    return tile


def column(row):
    d = row.shape[1]
    spread = jnp.broadcast_to(row, (d, d))
    eye = lax.broadcasted_iota(jnp.int32, (d, d), 0) == lax.broadcasted_iota(jnp.int32, (d, d), 1)
    return jnp.sum(jnp.where(eye, spread, 0.0), axis=1, keepdims=True)


def split3(value):
    high = value.astype(BF16).astype(F32)
    rest = value - high
    middle = rest.astype(BF16).astype(F32)
    return high, middle, rest - middle


def padded(parts):
    rows = jnp.concatenate(parts, axis=0)
    return jnp.concatenate([rows, jnp.zeros((K_ROWS - rows.shape[0], rows.shape[1]), F32)], axis=0)


def x_side(x, inverse):
    wide = (x.astype(F32) * inverse).astype(BF16).astype(F32)
    square = jnp.sum(wide * wide, axis=0, keepdims=True) * (-0.5 * LOG2E)
    ones = jnp.ones((3, x.shape[1]), F32)
    return jnp.transpose(padded([*split3(wide * LOG2E), *split3(square), ones])).astype(BF16)


def z_side(z, inverse):
    wide = (z.astype(F32) * inverse).astype(BF16).astype(F32)
    square = jnp.sum(wide * wide, axis=0, keepdims=True) * (-0.5 * LOG2E)
    ones = jnp.ones((3, z.shape[1]), F32)
    return padded([wide, wide, wide, ones, *split3(square)]).astype(BF16)


def stacked(solves, signs):
    return jnp.concatenate([solves.astype(F32), (2 * signs - 1).astype(F32)], axis=0).astype(BF16)


def kern_tiles(tile, inverse, x, z_ref, kern_ref, arrived=lambda index: None, beside=lambda target: None):
    left = x_side(x, inverse)
    for index in range(kern_ref.shape[1] // tile):
        arrived(index)
        target = slice(index * tile, (index + 1) * tile)
        right = z_side(z_ref[:, target], inverse)
        kern_ref[:, target] = jnp.exp2(jnp.dot(left, right, preferred_element_type=F32)).astype(BF16)
        beside(target)


def near_body(
    tile, length_hbm, x_hbm, z_hbm, solves_hbm, signs_hbm,
    kern_ref, z_ref, stack_ref, length_ref, x_ref, solves_ref, signs_ref, sems,
):
    columns = kern_ref.shape[1]
    first = (lax.axis_index("probe") % 2) * columns
    whole = pl.ds(pl.multiple_of(first, columns), columns)
    copies = [
        pltpu.make_async_copy(length_hbm, length_ref, sems.at[0]),
        pltpu.make_async_copy(x_hbm, x_ref, sems.at[1]),
    ]
    copies.append(pltpu.make_async_copy(z_hbm.at[:, whole], z_ref, sems.at[4]))
    copies.append(pltpu.make_async_copy(solves_hbm.at[:, whole], solves_ref, sems.at[2]))
    copies.append(pltpu.make_async_copy(signs_hbm.at[:, whole], signs_ref, sems.at[3]))
    for copy in copies:
        copy.start()
    copies[0].wait()
    copies[1].wait()

    def arrived(index):
        if index == 0:
            for copy in copies[2:]:
                copy.wait()

    def beside(target):
        stack_ref[: 2 * solves_ref.shape[0], target] = stacked(solves_ref[:, target], signs_ref[:, target])

    kern_tiles(tile, column(1.0 / length_ref[...]), x_ref[...], z_ref, kern_ref, arrived, beside)


def far_body(tile, length_ref, x_ref, z_ref, kern_ref):
    kern_tiles(tile, column(1.0 / length_ref[...]), x_ref[...], z_ref, kern_ref)


def kern_cost(rows, columns):
    return pl.CostEstimate(
        flops=2 * rows * columns * K_ROWS, bytes_accessed=2 * rows * columns, transcendentals=rows * columns
    )


def near_call(length, x, z, solves, signs, columns):
    rows, probes = x.shape[1], solves.shape[0]
    tile = tile_of(columns, 2048)
    operands = [pltpu.with_memory_space_constraint(value, pltpu.HBM) for value in (length, x, z, solves, signs)]
    return pl.pallas_call(
        functools.partial(near_body, tile),
        out_shape=(
            pltpu.VMEM((rows, columns), BF16),
            pltpu.VMEM((z.shape[0], columns), z.dtype),
            pltpu.VMEM((4 * probes, columns), BF16),
        ),
        in_specs=[HBM] * 5,
        out_specs=(VMEM,) * 3,
        scratch_shapes=[
            pltpu.VMEM(length.shape, length.dtype),
            pltpu.VMEM(x.shape, x.dtype),
            pltpu.VMEM((probes, columns), solves.dtype),
            pltpu.VMEM((probes, columns), signs.dtype),
            pltpu.SemaphoreType.DMA((5,)),
        ],
        compiler_params=pltpu.CompilerParams(vmem_limit_bytes=24 << 20),
        cost_estimate=kern_cost(rows, columns),
        name="kern_near",
    )(*operands)


def far_call(length, x, z):
    rows, columns = x.shape[1], z.shape[1]
    return pl.pallas_call(
        functools.partial(far_body, tile_of(columns, 2048)),
        out_shape=pltpu.VMEM((rows, columns), BF16),
        in_specs=[VMEM] * 3,
        out_specs=VMEM,
        compiler_params=pltpu.CompilerParams(vmem_limit_bytes=24 << 20),
        cost_estimate=kern_cost(rows, columns),
        name="kern_far",
    )(length, x, z)


def stack_body(tile, near_ref, solves_ref, signs_ref, stack_ref):
    del near_ref
    half, columns = stack_ref.shape[0] // 2, stack_ref.shape[1]
    first = (lax.axis_index("probe") % 2) * columns
    for start in range(0, columns, tile):
        source = pl.ds(pl.multiple_of(first + start, tile), tile)
        stack_ref[half:, start : start + tile] = stacked(solves_ref[:, source], signs_ref[:, source])


def stack_call(near, solves2, signs2):
    rows, columns = near.shape
    return pl.pallas_call(
        functools.partial(stack_body, tile_of(columns, 2048)),
        out_shape=jax.ShapeDtypeStruct((rows, columns), BF16),
        in_specs=[VMEM] * 3,
        input_output_aliases={0: 0},
        out_specs=VMEM,
        compiler_params=pltpu.CompilerParams(vmem_limit_bytes=16 << 20),
        cost_estimate=pl.CostEstimate(flops=4 * rows * columns, bytes_accessed=8 * rows * columns, transcendentals=0),
        name="stack",
    )(near, solves2, signs2)


def project_body(tile, kern_ref, stack_ref, own_ref, other_ref):
    total = None
    for start in range(0, kern_ref.shape[1], tile):
        target = slice(start, start + tile)
        term = lax.dot_general(
            kern_ref[:, target], stack_ref[:, target], (((1,), (1,)), ((), ())), preferred_element_type=F32
        )
        total = term if total is None else total + term
    total = jnp.transpose(total)
    half = total.shape[0] // 2
    own_ref[...] = total[:half]
    other_ref[...] = total[half:].astype(BF16)


def project_call(kern, stack):
    rows, columns = kern.shape
    half = stack.shape[0] // 2
    return pl.pallas_call(
        functools.partial(project_body, tile_of(columns, 2048)),
        out_shape=(jax.ShapeDtypeStruct((half, rows), F32), jax.ShapeDtypeStruct((half, rows), BF16)),
        in_specs=[VMEM] * 2,
        out_specs=(VMEM,) * 2,
        compiler_params=pltpu.CompilerParams(vmem_limit_bytes=24 << 20),
        cost_estimate=pl.CostEstimate(
            flops=4 * rows * columns * half, bytes_accessed=2 * rows * columns, transcendentals=0
        ),
        name="project",
    )(kern, stack)


def gradient_body(
    tile, p_size, noise_ref, length_ref, z_ref, stacks, projections, data, kerns, grad_ref, weighted_ref
):
    group = lax.axis_index("probe") // 2
    groups, halves = len(stacks), len(kerns)
    columns = grad_ref.shape[1]
    count = kerns[0].shape[0]
    dims = data[0].shape[0]
    inverse = column(1.0 / length_ref[...])
    factor = inverse * inverse / (noise_ref[...] * p_size)

    def in_order(values):
        if groups != 2:
            return values
        own, other = values
        return [jnp.where(group == 0, own, other), jnp.where(group == 0, other, own)]

    lefts, rows = [], []
    for half in range(halves):
        blocks = []
        for index in range(groups):
            parts = []
            for block in projections:
                value = block[half * groups + index].astype(F32)
                middle = value.shape[0] // 2
                parts += [value[middle:], value[:middle]]
            blocks.append(jnp.concatenate(parts, axis=0))
        lefts.append(jnp.transpose(jnp.concatenate(in_order(blocks), axis=0)).astype(BF16))
        x = data[half][...].astype(F32)
        rows.append(jnp.concatenate([x, jnp.ones((16, x.shape[1]), F32)], axis=0).astype(BF16))

    def weigh(index):
        target = slice(index * tile, (index + 1) * tile)
        stack = jnp.concatenate(in_order([ref[:, target].astype(F32) for ref in stacks]), axis=0).astype(BF16)
        for half in range(halves):
            coef = jnp.dot(lefts[half], stack, preferred_element_type=F32)
            weighted = (kerns[half][:, target].astype(F32) * coef).astype(BF16)
            weighted_ref[index % 2, half * count : (half + 1) * count, :] = weighted

    def reduce(index):
        target = slice(index * tile, (index + 1) * tile)
        total = None
        for half in range(halves):
            weighted = weighted_ref[index % 2, half * count : (half + 1) * count, :]
            term = jnp.dot(rows[half], weighted, preferred_element_type=F32)
            total = term if total is None else total + term
        z = z_ref[:, target].astype(F32)
        grad_ref[:, target] = ((total[:dims] - z * total[dims : dims + 1]) * factor).astype(grad_ref.dtype)

    tiles = columns // tile
    for index in range(tiles + 1):
        if index < tiles:
            weigh(index)
        if index > 0:
            reduce(index - 1)


def gradient_call(noise, length, z, stacks, projections, data, kerns, p_size, dtype):
    rows, columns = kerns[0].shape
    groups, halves = len(stacks), len(kerns)
    tile = tile_of(columns, 256)

    def body(noise_ref, length_ref, z_ref, *refs):
        refs = list(refs)
        take = lambda size: [refs.pop(0) for _ in range(size)]
        stack_refs, projection_refs, data_refs, kern_refs = take(groups), take(2), take(halves), take(halves)
        gradient_body(
            tile, p_size, noise_ref, length_ref, z_ref,
            stack_refs, projection_refs, data_refs, kern_refs, *refs,
        )

    return pl.pallas_call(
        body,
        out_shape=jax.ShapeDtypeStruct(z.shape, dtype),
        in_specs=[VMEM] * (3 + groups + 2 + 2 * halves),
        out_specs=VMEM,
        scratch_shapes=[pltpu.VMEM((2, halves * rows, tile), BF16)],
        compiler_params=pltpu.CompilerParams(vmem_limit_bytes=24 << 20),
        cost_estimate=pl.CostEstimate(
            flops=2 * halves * rows * columns * 128, bytes_accessed=2 * halves * rows * columns, transcendentals=0
        ),
        name="gradient",
    )(noise, length, z, *stacks, *projections, *data, *kerns)


def solution(mesh):
    dp, ind, probe = mesh.shape["dp"], mesh.shape["ind"], mesh.shape["probe"]
    groups = probe // 2
    halves = dp if dp <= 2 else 1
    core_swap = [(i, i ^ 1) for i in range(probe)]
    pairwise = ind & (ind - 1) == 0

    def cores(value):
        return lax.ppermute(value, "probe", core_swap)

    def from_group(shift):
        return [((i + 2 * shift) % probe, i) for i in range(probe)]

    def from_ind(shift):
        return [(i ^ shift if pairwise else (i + shift) % ind, i) for i in range(ind)]

    def on_device(data_x, inducing_z, lengthscale, noise_var, solves, probe_signs):
        columns = inducing_z.shape[1] // 2
        p_size = solves.shape[0] * probe
        length = lengthscale.reshape(1, -1)

        solves2, signs2 = cores(solves), cores(probe_signs)
        data = [data_x]
        for _ in range(halves - 1):
            data.append(lax.ppermute(data_x, "dp", [(i, 1 - i) for i in range(dp)]))
        kern, z, near = near_call(length, data_x, inducing_z, solves, probe_signs, columns)
        kerns = [kern]
        stack = stack_call(near, solves2, signs2)
        stacks = [stack]
        for shift in range(1, groups):
            stacks.append(lax.ppermute(stack, "probe", from_group(shift)))
        own, other = project_call(kern, stack)
        for x in data[1:]:
            kerns.append(far_call(length, x, z))

        part = (own + cores(other).astype(F32)).astype(BF16)
        peers = []
        for shift in range(1, ind):
            peers.append(lax.ppermute(part, "ind", from_ind(shift)))
        block = sum([p.astype(F32) for p in peers], part.astype(F32)).astype(BF16)

        blocks = []
        for half in range(halves):
            for shift in range(groups):
                pairs = []
                for d in range(dp):
                    for source, target in from_group(shift):
                        pairs.append(((d ^ half) * probe + source, d * probe + target))
                blocks.append(block if half == 0 and shift == 0 else lax.ppermute(block, ("dp", "probe"), pairs))
        own_blocks = jnp.stack(blocks)
        other_blocks = cores(own_blocks)

        whole = halves == dp
        grad = gradient_call(
            noise_var.reshape(1, 1), length, z, stacks, (own_blocks, other_blocks), data, kerns, p_size,
            BF16 if whole else F32,
        )
        if not whole:
            grad = lax.psum(grad, "dp").astype(BF16)
        far = cores(grad)
        lower = lax.axis_index("probe") % 2 == 0
        return jnp.concatenate(
            [jnp.where(lower, grad, far).astype(F32), jnp.where(lower, far, grad).astype(F32)], axis=1
        )

    return jax.shard_map(
        on_device,
        mesh=mesh,
        in_specs=(P(None, "dp"), P(None, "ind"), P(), P(), P("probe", "ind"), P("probe", "ind")),
        out_specs=P(None, "ind"),
        check_vma=False,
    )
```

```python
import functools
import math

import jax
import jax.numpy as jnp
from jax import lax
from jax.experimental import pallas as pl
from jax.experimental.pallas import tpu as pltpu
from jax.sharding import PartitionSpec as P

LOG2E = math.log2(math.e)
F32 = jnp.float32
BF16 = jnp.bfloat16
VMEM = pl.BlockSpec(memory_space=pltpu.VMEM)
HBM = pl.BlockSpec(memory_space=pltpu.HBM)
K_ROWS = 128


def tile_of(extent, limit):
    tile = min(extent, limit)
    while extent % tile:
        tile //= 2
    return tile


def column(row):
    d = row.shape[1]
    spread = jnp.broadcast_to(row, (d, d))
    eye = lax.broadcasted_iota(jnp.int32, (d, d), 0) == lax.broadcasted_iota(jnp.int32, (d, d), 1)
    return jnp.sum(jnp.where(eye, spread, 0.0), axis=1, keepdims=True)


def split3(value):
    high = value.astype(BF16).astype(F32)
    rest = value - high
    middle = rest.astype(BF16).astype(F32)
    return high, middle, rest - middle


def padded(parts):
    rows = jnp.concatenate(parts, axis=0)
    return jnp.concatenate([rows, jnp.zeros((K_ROWS - rows.shape[0], rows.shape[1]), F32)], axis=0)


def x_side(x, inverse):
    wide = (x.astype(F32) * inverse).astype(BF16).astype(F32)
    square = jnp.sum(wide * wide, axis=0, keepdims=True) * (-0.5 * LOG2E)
    ones = jnp.ones((3, x.shape[1]), F32)
    return jnp.transpose(padded([*split3(wide * LOG2E), *split3(square), ones])).astype(BF16)


def z_side(z, inverse):
    wide = (z.astype(F32) * inverse).astype(BF16).astype(F32)
    square = jnp.sum(wide * wide, axis=0, keepdims=True) * (-0.5 * LOG2E)
    ones = jnp.ones((3, z.shape[1]), F32)
    return padded([wide, wide, wide, ones, *split3(square)]).astype(BF16)


def stacked(solves, signs):
    return jnp.concatenate([solves.astype(F32), (2 * signs - 1).astype(F32)], axis=0).astype(BF16)


def kern_tiles(tile, inverse, x, z_ref, kern_ref, arrived=lambda index: None, beside=lambda target: None):
    left = x_side(x, inverse)
    for index in range(kern_ref.shape[1] // tile):
        arrived(index)
        target = slice(index * tile, (index + 1) * tile)
        right = z_side(z_ref[:, target], inverse)
        kern_ref[:, target] = jnp.exp2(jnp.dot(left, right, preferred_element_type=F32)).astype(BF16)
        beside(target)


def near_body(
    tile, length_hbm, x_hbm, z_hbm, solves_hbm, signs_hbm,
    kern_ref, z_ref, stack_ref, length_ref, x_ref, solves_ref, signs_ref, sems,
):
    columns = kern_ref.shape[1]
    first = (lax.axis_index("probe") % 2) * columns
    whole = pl.ds(pl.multiple_of(first, columns), columns)
    copies = [
        pltpu.make_async_copy(length_hbm, length_ref, sems.at[0]),
        pltpu.make_async_copy(x_hbm, x_ref, sems.at[1]),
    ]
    copies.append(pltpu.make_async_copy(z_hbm.at[:, whole], z_ref, sems.at[4]))
    copies.append(pltpu.make_async_copy(solves_hbm.at[:, whole], solves_ref, sems.at[2]))
    copies.append(pltpu.make_async_copy(signs_hbm.at[:, whole], signs_ref, sems.at[3]))
    for copy in copies:
        copy.start()
    copies[0].wait()
    copies[1].wait()

    def arrived(index):
        if index == 0:
            for copy in copies[2:]:
                copy.wait()

    def beside(target):
        stack_ref[: 2 * solves_ref.shape[0], target] = stacked(solves_ref[:, target], signs_ref[:, target])

    kern_tiles(tile, column(1.0 / length_ref[...]), x_ref[...], z_ref, kern_ref, arrived, beside)


def far_body(tile, length_ref, x_ref, z_ref, kern_ref):
    kern_tiles(tile, column(1.0 / length_ref[...]), x_ref[...], z_ref, kern_ref)


def kern_cost(rows, columns):
    return pl.CostEstimate(
        flops=2 * rows * columns * K_ROWS, bytes_accessed=2 * rows * columns, transcendentals=rows * columns
    )


def near_call(length, x, z, solves, signs, columns):
    rows, probes = x.shape[1], solves.shape[0]
    tile = tile_of(columns, 2048)
    operands = [pltpu.with_memory_space_constraint(value, pltpu.HBM) for value in (length, x, z, solves, signs)]
    return pl.pallas_call(
        functools.partial(near_body, tile),
        out_shape=(
            pltpu.VMEM((rows, columns), BF16),
            pltpu.VMEM((z.shape[0], columns), z.dtype),
            pltpu.VMEM((4 * probes, columns), BF16),
        ),
        in_specs=[HBM] * 5,
        out_specs=(VMEM,) * 3,
        scratch_shapes=[
            pltpu.VMEM(length.shape, length.dtype),
            pltpu.VMEM(x.shape, x.dtype),
            pltpu.VMEM((probes, columns), solves.dtype),
            pltpu.VMEM((probes, columns), signs.dtype),
            pltpu.SemaphoreType.DMA((5,)),
        ],
        compiler_params=pltpu.CompilerParams(vmem_limit_bytes=24 << 20),
        cost_estimate=kern_cost(rows, columns),
        name="kern_near",
    )(*operands)


def far_call(length, x, z):
    rows, columns = x.shape[1], z.shape[1]
    return pl.pallas_call(
        functools.partial(far_body, tile_of(columns, 2048)),
        out_shape=pltpu.VMEM((rows, columns), BF16),
        in_specs=[VMEM] * 3,
        out_specs=VMEM,
        compiler_params=pltpu.CompilerParams(vmem_limit_bytes=24 << 20),
        cost_estimate=kern_cost(rows, columns),
        name="kern_far",
    )(length, x, z)


def stack_body(tile, near_ref, solves_ref, signs_ref, stack_ref):
    del near_ref
    half, columns = stack_ref.shape[0] // 2, stack_ref.shape[1]
    first = (lax.axis_index("probe") % 2) * columns
    for start in range(0, columns, tile):
        source = pl.ds(pl.multiple_of(first + start, tile), tile)
        stack_ref[half:, start : start + tile] = stacked(solves_ref[:, source], signs_ref[:, source])


def stack_call(near, solves2, signs2):
    rows, columns = near.shape
    return pl.pallas_call(
        functools.partial(stack_body, tile_of(columns, 2048)),
        out_shape=jax.ShapeDtypeStruct((rows, columns), BF16),
        in_specs=[VMEM] * 3,
        input_output_aliases={0: 0},
        out_specs=VMEM,
        compiler_params=pltpu.CompilerParams(vmem_limit_bytes=16 << 20),
        cost_estimate=pl.CostEstimate(flops=4 * rows * columns, bytes_accessed=8 * rows * columns, transcendentals=0),
        name="stack",
    )(near, solves2, signs2)


def project_body(tile, kern_ref, stack_ref, own_ref, other_ref):
    total = None
    for start in range(0, kern_ref.shape[1], tile):
        target = slice(start, start + tile)
        term = lax.dot_general(
            kern_ref[:, target], stack_ref[:, target], (((1,), (1,)), ((), ())), preferred_element_type=F32
        )
        total = term if total is None else total + term
    total = jnp.transpose(total)
    half = total.shape[0] // 2
    own_ref[...] = total[:half]
    other_ref[...] = total[half:].astype(BF16)


def project_call(kern, stack):
    rows, columns = kern.shape
    half = stack.shape[0] // 2
    return pl.pallas_call(
        functools.partial(project_body, tile_of(columns, 2048)),
        out_shape=(jax.ShapeDtypeStruct((half, rows), F32), jax.ShapeDtypeStruct((half, rows), BF16)),
        in_specs=[VMEM] * 2,
        out_specs=(VMEM,) * 2,
        compiler_params=pltpu.CompilerParams(vmem_limit_bytes=24 << 20),
        cost_estimate=pl.CostEstimate(
            flops=4 * rows * columns * half, bytes_accessed=2 * rows * columns, transcendentals=0
        ),
        name="project",
    )(kern, stack)


def gradient_body(
    tile, p_size, noise_ref, length_ref, z_ref, stacks, projections, data, kerns, grad_ref, weighted_ref
):
    group = lax.axis_index("probe") // 2
    groups, halves = len(stacks), len(kerns)
    columns = grad_ref.shape[1]
    count = kerns[0].shape[0]
    dims = data[0].shape[0]
    inverse = column(1.0 / length_ref[...])
    factor = inverse * inverse / (noise_ref[...] * p_size)

    def in_order(values):
        if groups != 2:
            return values
        own, other = values
        return [jnp.where(group == 0, own, other), jnp.where(group == 0, other, own)]

    lefts, rows = [], []
    for half in range(halves):
        blocks = []
        for index in range(groups):
            parts = []
            for block in projections:
                value = block[half * groups + index].astype(F32)
                middle = value.shape[0] // 2
                parts += [value[middle:], value[:middle]]
            blocks.append(jnp.concatenate(parts, axis=0))
        lefts.append(jnp.transpose(jnp.concatenate(in_order(blocks), axis=0)).astype(BF16))
        x = data[half][...].astype(F32)
        rows.append(jnp.concatenate([x, jnp.ones((16, x.shape[1]), F32)], axis=0).astype(BF16))

    def weigh(index):
        target = slice(index * tile, (index + 1) * tile)
        stack = jnp.concatenate(in_order([ref[:, target].astype(F32) for ref in stacks]), axis=0).astype(BF16)
        for half in range(halves):
            coef = jnp.dot(lefts[half], stack, preferred_element_type=F32)
            weighted = (kerns[half][:, target].astype(F32) * coef).astype(BF16)
            weighted_ref[index % 2, half * count : (half + 1) * count, :] = weighted

    def reduce(index):
        target = slice(index * tile, (index + 1) * tile)
        total = None
        for half in range(halves):
            weighted = weighted_ref[index % 2, half * count : (half + 1) * count, :]
            term = jnp.dot(rows[half], weighted, preferred_element_type=F32)
            total = term if total is None else total + term
        z = z_ref[:, target].astype(F32)
        grad_ref[:, target] = ((total[:dims] - z * total[dims : dims + 1]) * factor).astype(grad_ref.dtype)

    tiles = columns // tile
    for index in range(tiles + 1):
        if index < tiles:
            weigh(index)
        if index > 0:
            reduce(index - 1)


def gradient_call(noise, length, z, stacks, projections, data, kerns, p_size, dtype):
    rows, columns = kerns[0].shape
    groups, halves = len(stacks), len(kerns)
    tile = tile_of(columns, 256)

    def body(noise_ref, length_ref, z_ref, *refs):
        refs = list(refs)
        take = lambda size: [refs.pop(0) for _ in range(size)]
        stack_refs, projection_refs, data_refs, kern_refs = take(groups), take(2), take(halves), take(halves)
        gradient_body(
            tile, p_size, noise_ref, length_ref, z_ref,
            stack_refs, projection_refs, data_refs, kern_refs, *refs,
        )

    return pl.pallas_call(
        body,
        out_shape=jax.ShapeDtypeStruct(z.shape, dtype),
        in_specs=[VMEM] * (3 + groups + 2 + 2 * halves),
        out_specs=VMEM,
        scratch_shapes=[pltpu.VMEM((2, halves * rows, tile), BF16)],
        compiler_params=pltpu.CompilerParams(vmem_limit_bytes=24 << 20),
        cost_estimate=pl.CostEstimate(
            flops=2 * halves * rows * columns * 128, bytes_accessed=2 * halves * rows * columns, transcendentals=0
        ),
        name="gradient",
    )(noise, length, z, *stacks, *projections, *data, *kerns)


def write_body(tile, other, grad_ref, *refs):
    out_ref, wide_ref, sems = refs[-3:]
    columns = grad_ref.shape[1]
    core = lax.axis_index("probe") % 2
    first = (1 - core if other else core) * columns
    copies = []
    for index in range(columns // tile):
        source = pl.ds(index * tile, tile)
        target = pl.ds(pl.multiple_of(first + index * tile, tile), tile)
        wide_ref[:, source] = grad_ref[:, source].astype(F32)
        copies.append(pltpu.make_async_copy(wide_ref.at[:, source], out_ref.at[:, target], sems.at[index]))
        copies[-1].start()
    for copy in copies:
        copy.wait()


def write_call(grad, out=None):
    rows, columns = grad.shape
    tile = tile_of(columns, 2048)
    other = out is not None
    return pl.pallas_call(
        functools.partial(write_body, tile, other),
        out_shape=jax.ShapeDtypeStruct((rows, 2 * columns), F32),
        in_specs=[VMEM] + [HBM] * other,
        out_specs=HBM,
        scratch_shapes=[pltpu.VMEM((rows, columns), F32), pltpu.SemaphoreType.DMA((columns // tile,))],
        input_output_aliases={1: 0} if other else {},
        compiler_params=pltpu.CompilerParams(vmem_limit_bytes=16 << 20),
        cost_estimate=pl.CostEstimate(flops=rows * columns, bytes_accessed=6 * rows * columns, transcendentals=0),
        name="write_other" if other else "write_own",
    )(grad, *([out] if other else []))


def solution(mesh):
    dp, ind, probe = mesh.shape["dp"], mesh.shape["ind"], mesh.shape["probe"]
    groups = probe // 2
    halves = dp if dp <= 2 else 1
    core_swap = [(i, i ^ 1) for i in range(probe)]
    pairwise = ind & (ind - 1) == 0

    def cores(value):
        return lax.ppermute(value, "probe", core_swap)

    def from_group(shift):
        return [((i + 2 * shift) % probe, i) for i in range(probe)]

    def from_ind(shift):
        return [(i ^ shift if pairwise else (i + shift) % ind, i) for i in range(ind)]

    def on_device(data_x, inducing_z, lengthscale, noise_var, solves, probe_signs):
        columns = inducing_z.shape[1] // 2
        p_size = solves.shape[0] * probe
        length = lengthscale.reshape(1, -1)

        solves2, signs2 = cores(solves), cores(probe_signs)
        data = [data_x]
        for _ in range(halves - 1):
            data.append(lax.ppermute(data_x, "dp", [(i, 1 - i) for i in range(dp)]))
        kern, z, near = near_call(length, data_x, inducing_z, solves, probe_signs, columns)
        kerns = [kern]
        stack = stack_call(near, solves2, signs2)
        stacks = [stack]
        for shift in range(1, groups):
            stacks.append(lax.ppermute(stack, "probe", from_group(shift)))
        own, other = project_call(kern, stack)
        for x in data[1:]:
            kerns.append(far_call(length, x, z))

        part = (own + cores(other).astype(F32)).astype(BF16)
        peers = []
        for shift in range(1, ind):
            peers.append(lax.ppermute(part, "ind", from_ind(shift)))
        block = sum([p.astype(F32) for p in peers], part.astype(F32)).astype(BF16)

        blocks = []
        for half in range(halves):
            for shift in range(groups):
                pairs = []
                for d in range(dp):
                    for source, target in from_group(shift):
                        pairs.append(((d ^ half) * probe + source, d * probe + target))
                blocks.append(block if half == 0 and shift == 0 else lax.ppermute(block, ("dp", "probe"), pairs))
        own_blocks = jnp.stack(blocks)
        other_blocks = cores(own_blocks)

        whole = halves == dp
        grad = gradient_call(
            noise_var.reshape(1, 1), length, z, stacks, (own_blocks, other_blocks), data, kerns, p_size,
            BF16 if whole else F32,
        )
        if not whole:
            grad = lax.psum(grad, "dp").astype(BF16)
        far = cores(grad)
        out = write_call(grad)
        return write_call(far, out)

    return jax.shard_map(
        on_device,
        mesh=mesh,
        in_specs=(P(None, "dp"), P(None, "ind"), P(), P(), P("probe", "ind"), P("probe", "ind")),
        out_specs=P(None, "ind"),
        check_vma=False,
    )
```

```python
import functools
import math

import jax
import jax.numpy as jnp
from jax import lax
from jax.experimental import pallas as pl
from jax.experimental.pallas import tpu as pltpu
from jax.sharding import PartitionSpec as P

LOG2E = math.log2(math.e)
F32 = jnp.float32
BF16 = jnp.bfloat16
VMEM = pl.BlockSpec(memory_space=pltpu.VMEM)
HBM = pl.BlockSpec(memory_space=pltpu.HBM)
K_ROWS = 128


def tile_of(extent, limit):
    tile = min(extent, limit)
    while extent % tile:
        tile //= 2
    return tile


def column(row):
    d = row.shape[1]
    spread = jnp.broadcast_to(row, (d, d))
    eye = lax.broadcasted_iota(jnp.int32, (d, d), 0) == lax.broadcasted_iota(jnp.int32, (d, d), 1)
    return jnp.sum(jnp.where(eye, spread, 0.0), axis=1, keepdims=True)


def split3(value):
    high = value.astype(BF16).astype(F32)
    rest = value - high
    middle = rest.astype(BF16).astype(F32)
    return high, middle, rest - middle


def padded(parts):
    rows = jnp.concatenate(parts, axis=0)
    return jnp.concatenate([rows, jnp.zeros((K_ROWS - rows.shape[0], rows.shape[1]), F32)], axis=0)


def x_side(x, inverse):
    wide = (x.astype(F32) * inverse).astype(BF16).astype(F32)
    square = jnp.sum(wide * wide, axis=0, keepdims=True) * (-0.5 * LOG2E)
    ones = jnp.ones((3, x.shape[1]), F32)
    return jnp.transpose(padded([*split3(wide * LOG2E), *split3(square), ones])).astype(BF16)


def z_side(z, inverse):
    wide = (z.astype(F32) * inverse).astype(BF16).astype(F32)
    square = jnp.sum(wide * wide, axis=0, keepdims=True) * (-0.5 * LOG2E)
    ones = jnp.ones((3, z.shape[1]), F32)
    return padded([wide, wide, wide, ones, *split3(square)]).astype(BF16)


def stacked(solves, signs):
    return jnp.concatenate([solves.astype(F32), (2 * signs - 1).astype(F32)], axis=0).astype(BF16)


def kern_tiles(tile, inverse, x, z_ref, kern_ref, arrived=lambda index: None, beside=lambda target: None):
    left = x_side(x, inverse)
    for index in range(kern_ref.shape[1] // tile):
        arrived(index)
        target = slice(index * tile, (index + 1) * tile)
        right = z_side(z_ref[:, target], inverse)
        kern_ref[:, target] = jnp.exp2(jnp.dot(left, right, preferred_element_type=F32)).astype(BF16)
        beside(target)


def near_body(
    tile, length_hbm, x_hbm, z_hbm, solves_hbm, signs_hbm,
    kern_ref, z_ref, stack_ref, length_ref, x_ref, solves_ref, signs_ref, sems,
):
    columns = kern_ref.shape[1]
    first = (lax.axis_index("probe") % 2) * columns
    whole = pl.ds(pl.multiple_of(first, columns), columns)
    copies = [
        pltpu.make_async_copy(length_hbm, length_ref, sems.at[0]),
        pltpu.make_async_copy(x_hbm, x_ref, sems.at[1]),
    ]
    copies.append(pltpu.make_async_copy(z_hbm.at[:, whole], z_ref, sems.at[4]))
    copies.append(pltpu.make_async_copy(solves_hbm.at[:, whole], solves_ref, sems.at[2]))
    copies.append(pltpu.make_async_copy(signs_hbm.at[:, whole], signs_ref, sems.at[3]))
    for copy in copies:
        copy.start()
    copies[0].wait()
    copies[1].wait()

    def arrived(index):
        if index == 0:
            for copy in copies[2:]:
                copy.wait()

    def beside(target):
        stack_ref[: 2 * solves_ref.shape[0], target] = stacked(solves_ref[:, target], signs_ref[:, target])

    kern_tiles(tile, column(1.0 / length_ref[...]), x_ref[...], z_ref, kern_ref, arrived, beside)


def far_body(tile, length_ref, x_ref, z_ref, kern_ref):
    kern_tiles(tile, column(1.0 / length_ref[...]), x_ref[...], z_ref, kern_ref)


def kern_cost(rows, columns):
    return pl.CostEstimate(
        flops=2 * rows * columns * K_ROWS, bytes_accessed=2 * rows * columns, transcendentals=rows * columns
    )


def near_call(length, x, z, solves, signs, columns):
    rows, probes = x.shape[1], solves.shape[0]
    tile = tile_of(columns, 2048)
    operands = [pltpu.with_memory_space_constraint(value, pltpu.HBM) for value in (length, x, z, solves, signs)]
    return pl.pallas_call(
        functools.partial(near_body, tile),
        out_shape=(
            pltpu.VMEM((rows, columns), BF16),
            pltpu.VMEM((z.shape[0], columns), z.dtype),
            pltpu.VMEM((4 * probes, columns), BF16),
        ),
        in_specs=[HBM] * 5,
        out_specs=(VMEM,) * 3,
        scratch_shapes=[
            pltpu.VMEM(length.shape, length.dtype),
            pltpu.VMEM(x.shape, x.dtype),
            pltpu.VMEM((probes, columns), solves.dtype),
            pltpu.VMEM((probes, columns), signs.dtype),
            pltpu.SemaphoreType.DMA((5,)),
        ],
        compiler_params=pltpu.CompilerParams(vmem_limit_bytes=24 << 20),
        cost_estimate=kern_cost(rows, columns),
        name="kern_near",
    )(*operands)


def far_call(length, x, z):
    rows, columns = x.shape[1], z.shape[1]
    return pl.pallas_call(
        functools.partial(far_body, tile_of(columns, 2048)),
        out_shape=pltpu.VMEM((rows, columns), BF16),
        in_specs=[VMEM] * 3,
        out_specs=VMEM,
        compiler_params=pltpu.CompilerParams(vmem_limit_bytes=24 << 20),
        cost_estimate=kern_cost(rows, columns),
        name="kern_far",
    )(length, x, z)


def stack_body(tile, near_ref, solves_ref, signs_ref, stack_ref):
    del near_ref
    half, columns = stack_ref.shape[0] // 2, stack_ref.shape[1]
    first = (lax.axis_index("probe") % 2) * columns
    for start in range(0, columns, tile):
        source = pl.ds(pl.multiple_of(first + start, tile), tile)
        stack_ref[half:, start : start + tile] = stacked(solves_ref[:, source], signs_ref[:, source])


def stack_call(near, solves2, signs2):
    rows, columns = near.shape
    return pl.pallas_call(
        functools.partial(stack_body, tile_of(columns, 2048)),
        out_shape=jax.ShapeDtypeStruct((rows, columns), BF16),
        in_specs=[VMEM] * 3,
        input_output_aliases={0: 0},
        out_specs=VMEM,
        compiler_params=pltpu.CompilerParams(vmem_limit_bytes=16 << 20),
        cost_estimate=pl.CostEstimate(flops=4 * rows * columns, bytes_accessed=8 * rows * columns, transcendentals=0),
        name="stack",
    )(near, solves2, signs2)


def project_body(tile, kern_ref, stack_ref, own_ref, other_ref):
    total = None
    for start in range(0, kern_ref.shape[1], tile):
        target = slice(start, start + tile)
        term = lax.dot_general(
            kern_ref[:, target], stack_ref[:, target], (((1,), (1,)), ((), ())), preferred_element_type=F32
        )
        total = term if total is None else total + term
    total = jnp.transpose(total)
    half = total.shape[0] // 2
    own_ref[...] = total[:half]
    other_ref[...] = total[half:].astype(BF16)


def project_call(kern, stack):
    rows, columns = kern.shape
    half = stack.shape[0] // 2
    return pl.pallas_call(
        functools.partial(project_body, tile_of(columns, 2048)),
        out_shape=(jax.ShapeDtypeStruct((half, rows), F32), jax.ShapeDtypeStruct((half, rows), BF16)),
        in_specs=[VMEM] * 2,
        out_specs=(VMEM,) * 2,
        compiler_params=pltpu.CompilerParams(vmem_limit_bytes=24 << 20),
        cost_estimate=pl.CostEstimate(
            flops=4 * rows * columns * half, bytes_accessed=2 * rows * columns, transcendentals=0
        ),
        name="project",
    )(kern, stack)


def gradient_body(
    tile, p_size, noise_ref, length_ref, z_ref, stacks, projections, data, kerns, grad_ref, weighted_ref
):
    group = lax.axis_index("probe") // 2
    groups, halves = len(stacks), len(kerns)
    columns = grad_ref.shape[1]
    count = kerns[0].shape[0]
    piece = tile_of(count, 256)
    dims = data[0].shape[0]
    inverse = column(1.0 / length_ref[...])
    factor = inverse * inverse / (noise_ref[...] * p_size)

    def in_order(values):
        if groups != 2:
            return values
        own, other = values
        return [jnp.where(group == 0, own, other), jnp.where(group == 0, other, own)]

    lefts, rows = [], []
    for half in range(halves):
        blocks = []
        for index in range(groups):
            parts = []
            for block in projections:
                value = block[half * groups + index].astype(F32)
                middle = value.shape[0] // 2
                parts += [value[middle:], value[:middle]]
            blocks.append(jnp.concatenate(parts, axis=0))
        lefts.append(jnp.transpose(jnp.concatenate(in_order(blocks), axis=0)).astype(BF16))
        x = data[half][...].astype(F32)
        rows.append(jnp.concatenate([x, jnp.ones((16, x.shape[1]), F32)], axis=0).astype(BF16))

    def weigh(index):
        target = slice(index * tile, (index + 1) * tile)
        stack = jnp.concatenate(in_order([ref[:, target].astype(F32) for ref in stacks]), axis=0).astype(BF16)
        for half in range(halves):
            for start in range(0, count, piece):
                part = slice(start, start + piece)
                coef = jnp.dot(lefts[half][part], stack, preferred_element_type=F32)
                weighted = (kerns[half][part, target].astype(F32) * coef).astype(BF16)
                weighted_ref[index % 2, half * count + start : half * count + start + piece, :] = weighted

    def reduce(index):
        target = slice(index * tile, (index + 1) * tile)
        total = None
        for half in range(halves):
            weighted = weighted_ref[index % 2, half * count : (half + 1) * count, :]
            term = jnp.dot(rows[half], weighted, preferred_element_type=F32)
            total = term if total is None else total + term
        z = z_ref[:, target].astype(F32)
        grad_ref[:, target] = ((total[:dims] - z * total[dims : dims + 1]) * factor).astype(grad_ref.dtype)

    tiles = columns // tile
    for index in range(tiles + 1):
        if index < tiles:
            weigh(index)
        if index > 0:
            reduce(index - 1)


def gradient_call(noise, length, z, stacks, projections, data, kerns, p_size, dtype):
    rows, columns = kerns[0].shape
    groups, halves = len(stacks), len(kerns)
    tile = tile_of(columns, 256)

    def body(noise_ref, length_ref, z_ref, *refs):
        refs = list(refs)
        take = lambda size: [refs.pop(0) for _ in range(size)]
        stack_refs, projection_refs, data_refs, kern_refs = take(groups), take(2), take(halves), take(halves)
        gradient_body(
            tile, p_size, noise_ref, length_ref, z_ref,
            stack_refs, projection_refs, data_refs, kern_refs, *refs,
        )

    return pl.pallas_call(
        body,
        out_shape=jax.ShapeDtypeStruct(z.shape, dtype),
        in_specs=[VMEM] * (3 + groups + 2 + 2 * halves),
        out_specs=VMEM,
        scratch_shapes=[pltpu.VMEM((2, halves * rows, tile), BF16)],
        compiler_params=pltpu.CompilerParams(vmem_limit_bytes=24 << 20),
        cost_estimate=pl.CostEstimate(
            flops=2 * halves * rows * columns * 128, bytes_accessed=2 * halves * rows * columns, transcendentals=0
        ),
        name="gradient",
    )(noise, length, z, *stacks, *projections, *data, *kerns)


def write_body(tile, other, grad_ref, *refs):
    out_ref, wide_ref, sems = refs[-3:]
    columns = grad_ref.shape[1]
    core = lax.axis_index("probe") % 2
    first = (1 - core if other else core) * columns
    copies = []
    for index in range(columns // tile):
        source = pl.ds(index * tile, tile)
        target = pl.ds(pl.multiple_of(first + index * tile, tile), tile)
        wide_ref[:, source] = grad_ref[:, source].astype(F32)
        copies.append(pltpu.make_async_copy(wide_ref.at[:, source], out_ref.at[:, target], sems.at[index]))
        copies[-1].start()
    for copy in copies:
        copy.wait()


def write_call(grad, out=None):
    rows, columns = grad.shape
    tile = tile_of(columns, 2048)
    other = out is not None
    return pl.pallas_call(
        functools.partial(write_body, tile, other),
        out_shape=jax.ShapeDtypeStruct((rows, 2 * columns), F32),
        in_specs=[VMEM] + [HBM] * other,
        out_specs=HBM,
        scratch_shapes=[pltpu.VMEM((rows, columns), F32), pltpu.SemaphoreType.DMA((columns // tile,))],
        input_output_aliases={1: 0} if other else {},
        compiler_params=pltpu.CompilerParams(vmem_limit_bytes=16 << 20),
        cost_estimate=pl.CostEstimate(flops=rows * columns, bytes_accessed=6 * rows * columns, transcendentals=0),
        name="write_other" if other else "write_own",
    )(grad, *([out] if other else []))


def solution(mesh):
    dp, ind, probe = mesh.shape["dp"], mesh.shape["ind"], mesh.shape["probe"]
    groups = probe // 2
    halves = dp if dp <= 2 else 1
    core_swap = [(i, i ^ 1) for i in range(probe)]
    pairwise = ind & (ind - 1) == 0

    def cores(value):
        return lax.ppermute(value, "probe", core_swap)

    def from_group(shift):
        return [((i + 2 * shift) % probe, i) for i in range(probe)]

    def from_ind(shift):
        return [(i ^ shift if pairwise else (i + shift) % ind, i) for i in range(ind)]

    def on_device(data_x, inducing_z, lengthscale, noise_var, solves, probe_signs):
        columns = inducing_z.shape[1] // 2
        p_size = solves.shape[0] * probe
        length = lengthscale.reshape(1, -1)

        solves2, signs2 = cores(solves), cores(probe_signs)
        data = [data_x]
        for _ in range(halves - 1):
            data.append(lax.ppermute(data_x, "dp", [(i, 1 - i) for i in range(dp)]))
        kern, z, near = near_call(length, data_x, inducing_z, solves, probe_signs, columns)
        kerns = [kern]
        stack = stack_call(near, solves2, signs2)
        stacks = [stack]
        for shift in range(1, groups):
            stacks.append(lax.ppermute(stack, "probe", from_group(shift)))
        own, other = project_call(kern, stack)
        for x in data[1:]:
            kerns.append(far_call(length, x, z))

        part = (own + cores(other).astype(F32)).astype(BF16)
        peers = []
        for shift in range(1, ind):
            peers.append(lax.ppermute(part, "ind", from_ind(shift)))
        block = sum([p.astype(F32) for p in peers], part.astype(F32)).astype(BF16)

        blocks = []
        for half in range(halves):
            for shift in range(groups):
                pairs = []
                for d in range(dp):
                    for source, target in from_group(shift):
                        pairs.append(((d ^ half) * probe + source, d * probe + target))
                blocks.append(block if half == 0 and shift == 0 else lax.ppermute(block, ("dp", "probe"), pairs))
        own_blocks = jnp.stack(blocks)
        other_blocks = cores(own_blocks)

        whole = halves == dp
        grad = gradient_call(
            noise_var.reshape(1, 1), length, z, stacks, (own_blocks, other_blocks), data, kerns, p_size,
            BF16 if whole else F32,
        )
        if not whole:
            grad = lax.psum(grad, "dp").astype(BF16)
        far = cores(grad)
        out = write_call(grad)
        return write_call(far, out)

    return jax.shard_map(
        on_device,
        mesh=mesh,
        in_specs=(P(None, "dp"), P(None, "ind"), P(), P(), P("probe", "ind"), P("probe", "ind")),
        out_specs=P(None, "ind"),
        check_vma=False,
    )
```
